32 devices in a mesh: row: 8 (over y, x, core), col: 4 (over z).
Axes of the slice: x: 2, y: 2, z: 4, core: 2. Of those that a mesh axis runs over, the one named last changes fastest.
Arguments:
- upper_s: float32 [4, 2048, 8, 1024], P(None, 'row', None, 'col')
- upper_t: float32 [4, 2048, 8, 1024], P(None, 'row', None, 'col')
- left_vectors: float32 [4, 2048, 8, 1024], P(None, 'row', None, 'col'), may hold values from -6 to 6
- right_vectors: float32 [4, 2048, 8, 1024], P(None, 'row', None, 'col'), may hold values from -6 to 6
- window_starts: int32 [3, 16], replicated, may hold values from 0 to 31, as said below
- selection: int32 [3, 16, 256], replicated, may hold values 0 or 1
- window_factors: float32 [3, 16, 2, 256, 256], P(None, 'row')
Outputs:
- new_s: float32 [4, 2048, 8, 1024], P(None, 'row', None, 'col')
- new_t: float32 [4, 2048, 8, 1024], P(None, 'row', None, 'col')
- new_left: float32 [4, 2048, 8, 1024], P(None, 'row', None, 'col')
- new_right: float32 [4, 2048, 8, 1024], P(None, 'row', None, 'col')
The draws below stay inside these ranges and needn't reach their ends.
Inputs may be any that keep to these rules, and one draw needn't show every extreme that they name: `window_starts`: within each round the 16 block numbers are distinct.
All inputs are finite; a program needn't handle non-finite values.
Results may differ from the reference program's by a relative error of at most 0.0001.
Values sent between devices are 32-bit elements; how exact they have to be, the bound alone decides.
No kernel may reach another device: no remote copies, remote signals or barrier semaphores. Data moves between devices by JAX's collectives and lax.ppermute only.
A program may use at most 192 MiB of HBM per device.

```python
import jax
import jax.numpy as jnp
from jax import lax

N = 8192
W = 256
NWIN = 16
ROUNDS = 3
BR = 4
BC = 8
N_ROW = 8
N_COL = 4


def draw_upper_s(key, part):
    values = jax.random.normal(jax.random.fold_in(key, 11), (N, N), jnp.float32)
    return jnp.triu(values).reshape(BR, N // BR, BC, N // BC)


def draw_upper_t(key, part):
    values = 0.5 * jax.random.normal(jax.random.fold_in(key, 23), (N, N), jnp.float32)
    lifted = jax.random.uniform(jax.random.fold_in(key, 29), (N,), jnp.float32, 1.0, 2.0)
    return (jnp.triu(values) + jnp.diag(lifted)).reshape(BR, N // BR, BC, N // BC)


def draw_window_starts(key, part):
    round_keys = jax.random.split(jax.random.fold_in(key, 37), ROUNDS)
    picked = jax.vmap(lambda round_key: jax.random.permutation(round_key, N // W)[:NWIN])(round_keys)
    return picked.astype(jnp.int32)


def draw_window_factors(key, part):
    values = jax.random.normal(jax.random.fold_in(key, 41), (ROUNDS, NWIN, 2, W, W), jnp.float32)
    basis, upper = jnp.linalg.qr(values)
    return basis.astype(jnp.float32)


def place_ends(result, own_key, low, top_value):
    longest = result.shape.index(max(result.shape))
    spots = []
    for shift in (0, 1):
        where = [jax.random.randint(jax.random.fold_in(own_key, axis), (), 0, length) for axis, length in enumerate(result.shape)]
        where[longest] = (where[longest] + shift) % result.shape[longest]
        spots.append(tuple(where))
    return result.at[spots[0]].set(low).at[spots[1]].set(top_value)


def level_of(stream_key, dims, pieces, low, largest):
    def one(dim, shards_of):
        draws = jax.random.uniform(jax.random.fold_in(jax.random.fold_in(stream_key, 6), dim), (shards_of,), jnp.float32, low / len(pieces), largest / len(pieces))
        return jnp.repeat(jnp.exp(draws), dims[dim] // shards_of).reshape((-1,) + (1,) * (len(dims) - dim - 1))

    level = one(*pieces[0])
    for cut in pieces[1:]:
        level = level * one(*cut)
    return level


def bell_draw(key, extent, spread, most, shards=(), held_as=jnp.bfloat16):
    result = jax.random.normal(key, extent, jnp.float32) * spread
    if len(shards) > 0:
        result = level_of(key, extent, shards, -0.22, 0.18) * result
    return jnp.clip(result, min=-most, max=most).astype(held_as)


def setup_inputs(seed: int = 0) -> dict:
    key_of = jax.random.split(jax.random.key(seed), 8)
    upper_s = draw_upper_s(jax.random.fold_in(key_of[7], 71), 0)
    upper_t = draw_upper_t(jax.random.fold_in(key_of[7], 71), 0)
    left_vectors = bell_draw(key_of[2], (BR, N_ROW * W, BC, N_COL * W), 1.0, 6.0, ((1, 8), (3, 4)), jnp.float32)
    right_vectors = bell_draw(key_of[3], (BR, N_ROW * W, BC, N_COL * W), 1.0, 6.0, ((1, 8), (3, 4)), jnp.float32)
    window_starts = draw_window_starts(jax.random.fold_in(key_of[7], 71), 0)
    selection = place_ends((jax.random.randint(key_of[5], (ROUNDS, NWIN, W), 0, 2) < 1).astype(jnp.int32), jax.random.fold_in(key_of[5], 1), 0, 1)
    window_factors = draw_window_factors(jax.random.fold_in(key_of[7], 71), 0)
    return dict(upper_s=upper_s, upper_t=upper_t, left_vectors=left_vectors, right_vectors=right_vectors, window_starts=window_starts, selection=selection, window_factors=window_factors)


def destinations(flags):
    flags = flags.astype(jnp.int32)
    earlier = (jnp.cumsum(flags) - flags).astype(jnp.int32)
    chosen = jnp.sum(flags).astype(jnp.int32)
    position = jnp.arange(flags.shape[0], dtype=jnp.int32)
    return jnp.where(flags == 1, earlier, chosen + position - earlier).astype(jnp.int32)

def window_bases(factors, flags):
    target = destinations(flags)
    return (jnp.take(factors[0], target, axis=0), jnp.take(factors[1], target, axis=0))

def product(left, right):
    return jnp.dot(left.astype(jnp.float32), right.astype(jnp.float32), precision=lax.Precision.HIGHEST, preferred_element_type=jnp.float32)

def reference(upper_s, upper_t, left_vectors, right_vectors, window_starts, selection, window_factors):
    mats = (upper_s.reshape(N, N), upper_t.reshape(N, N), left_vectors.reshape(N, N), right_vectors.reshape(N, N))
    for round_idx in range(ROUNDS):

        def apply_window(index, state):
            pencil_s, pencil_t, left_basis, right_basis = state
            left_factor, right_factor = window_bases(window_factors[round_idx, index], selection[round_idx, index])
            offset = (window_starts[round_idx, index] * W).astype(jnp.int32)
            band_s = lax.dynamic_slice_in_dim(pencil_s, offset, W, 0)
            pencil_s = lax.dynamic_update_slice_in_dim(pencil_s, product(left_factor.T, band_s), offset, 0)
            band_t = lax.dynamic_slice_in_dim(pencil_t, offset, W, 0)
            pencil_t = lax.dynamic_update_slice_in_dim(pencil_t, product(left_factor.T, band_t), offset, 0)
            strip_s = lax.dynamic_slice_in_dim(pencil_s, offset, W, 1)
            pencil_s = lax.dynamic_update_slice_in_dim(pencil_s, product(strip_s, right_factor), offset, 1)
            strip_t = lax.dynamic_slice_in_dim(pencil_t, offset, W, 1)
            pencil_t = lax.dynamic_update_slice_in_dim(pencil_t, product(strip_t, right_factor), offset, 1)
            strip_left = lax.dynamic_slice_in_dim(left_basis, offset, W, 1)
            left_basis = lax.dynamic_update_slice_in_dim(left_basis, product(strip_left, left_factor), offset, 1)
            strip_right = lax.dynamic_slice_in_dim(right_basis, offset, W, 1)
            right_basis = lax.dynamic_update_slice_in_dim(right_basis, product(strip_right, right_factor), offset, 1)
            return (pencil_s, pencil_t, left_basis, right_basis)
        mats = lax.fori_loop(0, NWIN, apply_window, mats)
    return tuple((matrix.reshape(BR, N // BR, BC, N // BC) for matrix in mats))
```

```python
import functools
import math

import jax
import jax.numpy as jnp
import numpy as np
from jax import lax
from jax.experimental import pallas as pl
from jax.experimental.pallas import tpu as pltpu
from jax.sharding import PartitionSpec as P


F32 = jnp.float32
BF16 = jnp.bfloat16
LANES = 128
MIB = 1 << 20
ANY = pl.BlockSpec(memory_space=pl.ANY)
SMEM = pl.BlockSpec(memory_space=pltpu.SMEM)
VMEM = pl.BlockSpec(memory_space=pltpu.VMEM)


def halves(x):
    high = x.astype(BF16)
    return high, (x - high.astype(F32)).astype(BF16)


def dot(a, b):
    return jnp.dot(a, b, preferred_element_type=F32)


def dot_nt(a, b):
    return lax.dot_general(a, b, (((1,), (1,)), ((), ())), preferred_element_type=F32)


def product(a, b):
    return dot(a[0], b[0]) + (dot(a[0], b[1]) + dot(a[1], b[0]))


class Plan:
    def __init__(self, rows, cols, row_blocks, col_blocks, rounds, own, width):
        assert rows >= 4 and rows & (rows - 1) == 0
        self.rows, self.cols, self.row_blocks, self.col_blocks = rows, cols, row_blocks, col_blocks
        self.rounds, self.own, self.width, self.parts = rounds, own, width, width // LANES
        self.blocks = row_blocks * rows
        self.nodes = rows // 2
        self.stages = self.nodes.bit_length() - 1
        self.col_units = max(1, col_blocks // self.nodes)
        self.row_units = -(-row_blocks // cols)
        self.units = self.col_units + self.row_units
        self.slots = self.nodes * self.units * rounds
        self.most = [(self.nodes >> (t + 1)) * self.units * rounds for t in range(self.stages)]
        means = [m * own * rows / self.blocks * 2**t / self.nodes for t, m in enumerate(self.most)]
        self.cap = [min(m, max(1, math.ceil(x + 2.5 * math.sqrt(x)))) for m, x in zip(self.most, means)]

    def bit(self, t, core):
        return jnp.where(core == 0, 1 << (t % self.stages), 1 << ((t + 1) % self.stages))

    def mask(self, first, last, core):
        total = 0
        for t in range(first, last):
            total = total + self.bit(t, core)
        return total

    def turn(self, t):
        pairs = []
        for row in range(self.rows):
            shift = t % self.stages if row % 2 == 0 else (t + 1) % self.stages
            pairs.append((row, row ^ (2 << shift)))
        return pairs

    def swap(self):
        return [(row, row ^ 1) for row in range(self.rows)]

    def block_of(self, node, unit, core, col):
        first = ((node * self.col_blocks) // self.nodes + unit) * self.cols + col
        part = col * self.row_units + unit - self.col_units
        second = part * self.rows + 2 * node + core
        is_col = unit < self.col_units
        return is_col, jnp.where(is_col, first, jnp.clip(second, 0, self.blocks - 1)), is_col | (part < self.row_blocks)

    def present(self, t, here, node, owner, core):
        diff, away = node ^ here, owner ^ here
        ahead = (diff & self.mask(0, t, core)) == 0
        return ahead & ((diff & self.bit(t, core)) != 0) & ((away & self.mask(t, self.stages, core)) == 0)

    def overflows(self, starts):
        axes = (self.stages, 2, self.cols, self.nodes)
        stage, core, col, here = (x.reshape(-1, 1) for x in np.indices(axes).astype(np.int32))
        bits = np.array([[1 << ((t + c) % self.stages) for c in range(2)] for t in range(self.stages)], np.int32)
        before = np.array([[bits[:t, c].sum() for c in range(2)] for t in range(self.stages)], np.int32)[stage, core]
        now, after = bits[stage, core], (self.nodes - 1) & ~before
        block = starts.reshape(1, -1)
        windows = jnp.arange(starts.shape[1], dtype=jnp.int32) // (2 * self.own)
        owner = jnp.tile(windows, starts.shape[0]).reshape(1, -1)
        mine = ((owner ^ here) & after) == 0
        copies = max(1, self.nodes // self.col_blocks)
        total = 0
        for copy in range(copies):
            node = (block // self.cols // self.col_units) * copies + copy
            on = (block % self.cols == col) & (((node ^ here) & before) == 0) & (((node ^ here) & now) != 0)
            total = total + (on & mine).astype(jnp.int32)
        row, part = block % self.rows, block // self.rows
        node = row // 2
        on = (part // self.row_units == col) & (row % 2 == core)
        on = on & (((node ^ here) & before) == 0) & (((node ^ here) & now) != 0)
        total = total + (on & mine).astype(jnp.int32)
        counts = jnp.sum(total, axis=1).reshape(self.stages, -1)
        return jnp.max(counts, axis=1) > jnp.array(self.cap, jnp.int32)


SHIFT = 12


class Walk:
    def __init__(self, plan, meta, inv, stage, table):
        self.plan, self.inv, self.stage = plan, inv, stage
        self.row, self.col = meta[0], meta[1]
        self.core, self.here = self.row % 2, self.row // 2
        self.table = table
        for t in range(stage):
            self.scan(t, self.here ^ plan.bit(t, self.core), functools.partial(self.note, t))

    def note(self, t, slot, count, info):
        self.table[t, slot] = count

    def info(self, slot):
        plan = self.plan
        node = slot // (plan.units * plan.rounds)
        unit = (slot // plan.rounds) % plan.units
        turn = slot % plan.rounds
        is_col, block, valid = plan.block_of(node, unit, self.core, self.col)
        window = jnp.where(valid, self.inv[turn, block], -1)
        side = jnp.where(is_col, self.core, 0)
        return node, turn, window, side

    def scan(self, t, here, act):
        def step(slot, count):
            info = self.info(slot)
            owner = jnp.maximum(info[2], 0) // (2 * self.plan.own)
            hit = (info[2] >= 0) & self.plan.present(t, here, info[0], owner, self.core)

            @pl.when(hit)
            def _():
                act(slot, count, info)

            return count + hit.astype(jnp.int32)

        return lax.fori_loop(0, self.plan.slots, step, jnp.int32(0))

    def source(self, slot, info):
        plan = self.plan
        _, turn, window, side = info
        row = window // plan.own
        away = (row // 2) ^ self.here
        code = ((row != self.row).astype(jnp.int32) << SHIFT) + (turn * plan.own + window % plan.own) * 2 + side
        for t in range(self.stage):
            place = self.table[t, slot]
            rest = place >= plan.cap[t]
            there = ((2 + 2 * t + rest.astype(jnp.int32)) << SHIFT) + place - jnp.where(rest, plan.cap[t], 0)
            code = jnp.where((away & plan.bit(t, self.core)) != 0, there, code)
        return code


def route_kernel(plan, t, meta, inv, jobs, table):
    walk = Walk(plan, meta, inv, t, table)
    if t < plan.stages:

        def act(slot, count, info):
            jobs[1 + count] = walk.source(slot, info)

        jobs[0] = walk.scan(t, walk.here, act)
        return
    places = plan.units * plan.rounds

    def step(place, carry):
        slot = walk.here * places + place
        info = walk.info(slot)
        jobs[places + place] = info[2]
        jobs[place] = walk.source(slot, (info[0], info[1], jnp.maximum(info[2], 0), info[3]))
        return carry

    lax.fori_loop(0, places, step, 0)


def route(plan, t, meta, inv):
    size = 1 + plan.most[t] if t < plan.stages else 2 * plan.units * plan.rounds
    return pl.pallas_call(
        functools.partial(route_kernel, plan, t),
        in_specs=[SMEM, SMEM],
        out_specs=SMEM,
        out_shape=jax.ShapeDtypeStruct((size,), jnp.int32),
        scratch_shapes=[pltpu.SMEM((max(1, t), plan.slots), jnp.int32)],
        compiler_params=pltpu.CompilerParams(vmem_limit_bytes=MIB),
    )(meta, inv)


def fetch(code, sources, target, sem):
    for number, ref in enumerate(sources):

        @pl.when((code >> SHIFT) == number)
        def _(ref=ref):
            pltpu.make_async_copy(ref.at[code & ((1 << SHIFT) - 1)], target, sem).start()


def arrived(sources, target, sem):
    pltpu.make_async_copy(sources[0].at[0], target, sem).wait()


def pack_kernel(plan, t, jobs, *refs):
    sources, (first, rest, spill, sems, spill_sem) = refs[: 2 + 2 * t], refs[2 + 2 * t :]
    cap = plan.cap[t]
    count = jobs[0]

    def begin(place, carry):
        fetch(jobs[1 + place], sources, first.at[place], sems.at[place])
        return carry

    def settle(place, carry):
        arrived(sources, first.at[place], sems.at[place])
        return carry

    def over(place, carry):
        fetch(jobs[1 + place], sources, spill, spill_sem.at[0])
        arrived(sources, spill, spill_sem.at[0])
        out = pltpu.make_async_copy(spill, rest.at[place - cap], spill_sem.at[1])
        out.start()
        out.wait()
        return carry

    lax.fori_loop(0, jnp.minimum(count, cap), begin, 0)
    lax.fori_loop(cap, count, over, 0)
    lax.fori_loop(0, jnp.minimum(count, cap), settle, 0)


def pack(plan, t, jobs, sources):
    w, cap, rest = plan.width, plan.cap[t], max(1, plan.most[t] - plan.cap[t])
    return pl.pallas_call(
        functools.partial(pack_kernel, plan, t),
        in_specs=[SMEM] + [ANY] * len(sources),
        out_specs=[VMEM, ANY],
        out_shape=[jax.ShapeDtypeStruct((cap, w, w), F32), jax.ShapeDtypeStruct((rest, w, w), F32)],
        scratch_shapes=[
            pltpu.VMEM((w, w), F32),
            pltpu.SemaphoreType.DMA((cap,)),
            pltpu.SemaphoreType.DMA((2,)),
        ],
        compiler_params=pltpu.CompilerParams(vmem_limit_bytes=4 * MIB),
    )(jobs, *placed(sources))


def order(flags):
    width = flags.shape[1]
    row = lax.broadcasted_iota(jnp.int32, (width, width), 0)
    column = lax.broadcasted_iota(jnp.int32, (width, width), 1)
    wide = jnp.broadcast_to(flags, (8, width))
    earlier = dot(wide.astype(BF16), (row < column).astype(F32).astype(BF16))[0:1]
    chosen = jnp.sum(flags, axis=1, keepdims=True)
    position = lax.broadcasted_iota(jnp.int32, (1, width), 1).astype(F32)
    target = jnp.where(flags == 1.0, earlier, chosen + position - earlier)
    return (row.astype(F32) == target).astype(F32).astype(BF16)


def orders_kernel(plan, jobs, flags, out):
    places = plan.units * plan.rounds

    def step(place, carry):
        window = jnp.maximum(jobs[places + place], 0)
        out[place] = order(flags[place % plan.rounds, pl.ds(window, 1), :].astype(F32))
        return carry

    lax.fori_loop(0, places, step, 0)


def orders(plan, jobs, flags):
    return pl.pallas_call(
        functools.partial(orders_kernel, plan),
        in_specs=[SMEM, VMEM],
        out_specs=VMEM,
        out_shape=jax.ShapeDtypeStruct((plan.units * plan.rounds, plan.width, plan.width), BF16),
        compiler_params=pltpu.CompilerParams(vmem_limit_bytes=4 * MIB),
        name="orders",
    )(jobs, flags)


def compose_kernel(plan, jobs, moves, *refs):
    count = 2 + 2 * plan.stages
    sources, (cols, lefts, raw, held, sems) = refs[:count], refs[count:]
    w = plan.width
    places = plan.units * plan.rounds
    for turn in range(plan.rounds):
        for unit in range(plan.units):
            place = unit * plan.rounds + turn

            @pl.when(jobs[places + place] >= 0)
            def _(place=place):
                fetch(jobs[place], sources, raw.at[place], sems.at[place])

    row = lax.broadcasted_iota(jnp.int32, (w, w), 0)
    column = lax.broadcasted_iota(jnp.int32, (w, w), 1)
    unit_matrix = (row == column).astype(F32)
    for turn in range(plan.rounds):
        for unit in range(plan.units):
            place = unit * plan.rounds + turn

            @pl.when(jobs[places + place] >= 0)
            def _(place=place):
                arrived(sources, raw.at[place], sems.at[place])

        for unit in range(plan.units):
            place = unit * plan.rounds + turn
            there = jobs[places + place] >= 0
            factor = halves(jnp.where(there, raw[place], 0.0))
            if turn == 0:
                moved = dot_nt(unit_matrix.astype(BF16), moves[place]).astype(BF16)
                held[unit] = jnp.where(there, dot(moved, factor[0]) + dot(moved, factor[1]), unit_matrix)
            else:
                high, low = halves(held[unit])
                moved = dot_nt(high, moves[place]) + dot_nt(low, moves[place])
                held[unit] = jnp.where(there, product(halves(moved), factor), held[unit])

    for unit in range(plan.col_units):
        cols[unit] = held[unit]
    for unit in range(plan.row_units):
        lefts[unit] = held[plan.col_units + unit]


def compose(plan, jobs, moves, sources):
    w = plan.width
    return pl.pallas_call(
        functools.partial(compose_kernel, plan),
        in_specs=[SMEM, VMEM] + [ANY] * len(sources),
        out_specs=[VMEM, VMEM],
        out_shape=[
            jax.ShapeDtypeStruct((plan.col_units, w, w), F32),
            jax.ShapeDtypeStruct((plan.row_units, w, w), F32),
        ],
        scratch_shapes=[
            pltpu.VMEM((plan.units * plan.rounds, w, w), F32),
            pltpu.VMEM((plan.units, w, w), F32),
            pltpu.SemaphoreType.DMA((plan.units * plan.rounds,)),
        ],
        compiler_params=pltpu.CompilerParams(vmem_limit_bytes=8 * MIB),
        name="compose",
    )(jobs, moves, *placed(sources))


def tiles(plan, act):
    count = plan.row_blocks * plan.col_blocks * plan.parts

    def step(index, carry):
        a, rest = index // (plan.col_blocks * plan.parts), index % (plan.col_blocks * plan.parts)
        act(a, rest // plan.parts, rest % plan.parts)
        return carry

    lax.fori_loop(0, count, step, 0)


def hbm_piece(ref, a, b, p):
    return ref.at[a, :, p, b, 0]


def vmem_piece(ref, a, b, p):
    return ref.at[a, b, :, pl.ds(pl.multiple_of(p * LANES, LANES), LANES)]


def stage_kernel(plan, count, *refs):
    inputs, held, sems = refs[:count], refs[count : 2 * count], refs[2 * count]
    for start in (True, False):
        for m in range(count):

            def act(a, b, p, m=m):
                copy = pltpu.make_async_copy(hbm_piece(inputs[m], a, b, p), vmem_piece(held[m], a, b, p), sems.at[m])
                copy.start() if start else copy.wait()

            tiles(plan, act)


def stage(plan, inputs):
    shape = (plan.row_blocks, plan.col_blocks, plan.width, plan.width)
    count = len(inputs)
    return pl.pallas_call(
        functools.partial(stage_kernel, plan, count),
        in_specs=[ANY] * count,
        out_specs=[VMEM] * count,
        out_shape=[pltpu.VMEM(shape, F32)] * count,
        scratch_shapes=[pltpu.SemaphoreType.DMA((count,))],
        compiler_params=pltpu.CompilerParams(vmem_limit_bytes=MIB),
    )(*in_hbm(inputs))


def combine(plan, m, core):
    offset = 0
    for t in range(plan.stages):
        if (m >> t) & 1:
            offset = offset ^ plan.bit(t, core)
    return offset


def write_out(plan, source, target, b, sem):
    def step(index, carry):
        a, p = index // plan.parts, index % plan.parts
        pltpu.make_async_copy(vmem_piece(source, a, b, p), hbm_piece(target, a, b, p), sem).start()
        return carry

    lax.fori_loop(0, plan.row_blocks * plan.parts, step, 0)


def settle_out(plan, source, target, count, sem):
    def step(index, carry):
        pltpu.make_async_copy(vmem_piece(source, 0, 0, 0), hbm_piece(target, 0, 0, 0), sem).wait()
        return carry

    lax.fori_loop(0, count * plan.row_blocks * plan.parts, step, 0)


def columns(plan, masks, meta, gathered, swapped, data, outputs, high, low, places, sem):
    core, here = meta[0] % 2, meta[0] // 2
    count = jnp.int32(0)
    slots = {}
    for index, m in enumerate(masks):
        node = here ^ combine(plan, m, core)
        base = (node * plan.col_blocks) // plan.nodes
        whole = (node * plan.col_blocks) % plan.nodes == 0
        for unit in range(plan.col_units):
            places[count] = base + unit
            slots[index, unit] = count
            h, l = halves(gathered[index][unit])
            high[core, base + unit] = h
            low[core, base + unit] = l
            count = count + whole.astype(jnp.int32)
        other = here ^ combine(plan, m, 1 - core)
        base = (other * plan.col_blocks) // plan.nodes
        for unit in range(plan.col_units):
            h, l = halves(swapped[index][unit])
            high[1 - core, base + unit] = h
            low[1 - core, base + unit] = l

    def step(index, carry):
        b = places[index]
        for m, kind in ((2, 0), (3, 1), (0, 1), (1, 1)):
            ref = data[m]
            for a in range(plan.row_blocks):
                ref[a, b] = product(halves(ref[a, b]), (high[kind, b], low[kind, b]))
            if m >= 2:
                write_out(plan, ref, outputs[m - 2], b, sem)
        return carry

    lax.fori_loop(0, count, step, 0)
    return count


def early_kernel(plan, masks, extra, meta, *refs):
    n = len(masks)
    gathered, swapped, refs = refs[:n], refs[n : 2 * n], refs[2 * n + 4 + extra :]
    data, outputs, (high, low, places, sem) = refs[:4], refs[4:6], refs[6:]
    count = columns(plan, masks, meta, gathered, swapped, data, outputs, high, low, places, sem)
    settle_out(plan, data[2], outputs[0], 2 * count, sem)


def late_kernel(plan, masks, meta, *refs):
    n, br = len(masks), plan.row_blocks
    gathered, swapped, refs = refs[:n], refs[n : 2 * n], refs[2 * n :]
    lefts, refs = refs[: plan.cols], refs[plan.cols + 6 :]
    data, outputs, refs = refs[:4], refs[4:8], refs[8:]
    high, low, places, left, sem = refs
    w = plan.width
    for shift in range(plan.cols):
        origin = (meta[1] + plan.cols - shift) % plan.cols
        for unit in range(plan.row_units):
            place = origin * plan.row_units + unit

            @pl.when(place < br)
            def _(shift=shift, unit=unit, place=place):
                h, l = halves(lefts[shift][unit].T)
                left[place, pl.ds(0, plan.width)] = h
                left[place, pl.ds(plan.width, plan.width)] = l

    count = columns(plan, masks, meta, gathered, swapped, data, outputs[:2], high, low, places, sem)

    def rows(b, carry):
        for m in range(2):
            for a in range(br):
                y = halves(data[m][a, b])
                both = dot(left[a], y[0])
                data[m][a, b] = both[:w] + (both[w:] + dot(left[a, :w], y[1]))
            write_out(plan, data[m], outputs[2 + m], b, sem)
        return carry

    lax.fori_loop(0, plan.col_blocks, rows, 0)
    settle_out(plan, data[0], outputs[2], 2 * count + 2 * plan.col_blocks, sem)


def held_in_vmem(xs):
    return [pltpu.with_memory_space_constraint(x, pltpu.VMEM) for x in xs]


def placed(sources):
    spaces = [pltpu.VMEM if i >= 2 and i % 2 == 0 else pltpu.HBM for i in range(len(sources))]
    return [pltpu.with_memory_space_constraint(x, space) for x, space in zip(sources, spaces)]


def in_hbm(xs):
    return [pltpu.with_memory_space_constraint(x, pltpu.HBM) for x in xs]


def scratch(plan, limit):
    w, bc = plan.width, plan.col_blocks
    return [
        pltpu.VMEM((2, bc, w, w), BF16),
        pltpu.VMEM((2, bc, w, w), BF16),
        pltpu.SMEM((limit + 1,), jnp.int32),
    ]


def early(plan, masks, meta, gathered, swapped, data, shape, outputs):
    n = len(masks)
    held = [pltpu.VMEM(data[0].shape, F32)] * 4
    return pl.pallas_call(
        functools.partial(early_kernel, plan, masks, len(outputs)),
        in_specs=[SMEM] + [VMEM] * (2 * n + 4) + [ANY] * len(outputs),
        out_specs=[VMEM] * 4 + [ANY] * 2,
        out_shape=held + [jax.ShapeDtypeStruct(shape, F32)] * 2,
        input_output_aliases={1 + 2 * n + i: i for i in range(4 + len(outputs))},
        scratch_shapes=scratch(plan, n * plan.col_units) + [pltpu.SemaphoreType.DMA(())],
        compiler_params=pltpu.CompilerParams(vmem_limit_bytes=8 * MIB),
    )(meta, *gathered, *swapped, *held_in_vmem(data), *in_hbm(outputs))


def late(plan, masks, meta, gathered, swapped, lefts, data, outputs):
    n, w = len(masks), plan.width
    first = 1 + 2 * n + len(lefts)
    held = [pltpu.VMEM(data[0].shape, F32)] * 4
    shape = jax.ShapeDtypeStruct(outputs[0].shape, F32)
    return pl.pallas_call(
        functools.partial(late_kernel, plan, masks),
        in_specs=[SMEM] + [VMEM] * (2 * n + len(lefts) + 4) + [ANY] * 2,
        out_specs=[VMEM] * 4 + [ANY] * 4,
        out_shape=held + [shape] * 4,
        input_output_aliases={first + i: i for i in range(6)},
        scratch_shapes=scratch(plan, n * plan.col_units)
        + [pltpu.VMEM((plan.row_blocks, 2 * w, w), BF16)]
        + [pltpu.SemaphoreType.DMA(())],
        compiler_params=pltpu.CompilerParams(vmem_limit_bytes=8 * MIB),
        name="late",
    )(meta, *gathered, *swapped, *lefts, *held_in_vmem(data), *in_hbm(outputs))[4:]


def flat(x):
    a, q, b, m = x.shape
    return x.reshape(a, q, b, m // LANES, LANES).transpose(0, 1, 3, 2, 4).reshape(a, q, m // LANES, b, 1, LANES)


def unflat(y, shape):
    a, q, b, m = shape
    return y.reshape(a, q, m // LANES, b, LANES).transpose(0, 1, 3, 2, 4).reshape(shape)


def shards(upper_s, upper_t, left_vectors, right_vectors, window_starts, selection, window_factors):
    rows, cols = lax.axis_size("row"), lax.axis_size("col")
    shape = upper_s.shape
    plan = Plan(rows, cols, shape[0], shape[2], window_starts.shape[0], window_factors.shape[1], shape[1])
    meta = jnp.stack([lax.axis_index("row"), lax.axis_index("col")]).astype(jnp.int32)
    numbers = jnp.arange(plan.blocks, dtype=jnp.int32)
    windows = jnp.arange(window_starts.shape[1], dtype=jnp.int32)
    same = window_starts[:, None, :] == numbers[None, :, None]
    inv = jnp.sum(jnp.where(same, windows + 1, 0), axis=2) - 1
    over = plan.overflows(window_starts)

    inputs = [flat(x) for x in (upper_s, upper_t, left_vectors, right_vectors)]
    return steps(plan, meta, inv, over, inputs, shape, selection, window_factors)


def steps(plan, meta, inv, over, inputs, shape, selection, window_factors):
    cols = plan.cols
    held = stage(plan, inputs[:2]) + stage(plan, inputs[2:])
    window_factors = window_factors.reshape((-1,) + window_factors.shape[3:])
    sources = [window_factors, lax.ppermute(window_factors, "row", plan.swap())]
    for t in range(plan.stages):
        first, rest = pack(plan, t, route(plan, t, meta, inv), sources)
        sent = functools.partial(lax.ppermute, axis_name="row", perm=plan.turn(t))
        moved = sent(first)
        sources += [moved, lax.cond(over[t], sent, lambda x: x, rest)]
    jobs = route(plan, plan.stages, meta, inv)
    moves = orders(plan, jobs, selection)
    made, left = compose(plan, jobs, moves, sources)

    lefts = [left]
    for shift in range(1, cols):
        lefts.append(lax.ppermute(left, "col", [(c, (c + shift) % cols) for c in range(cols)]))
    gathered = [made]
    swapped = [lax.ppermute(made, "row", plan.swap())]
    for t in range(plan.stages):
        gathered += [lax.ppermute(x, "row", plan.turn(t)) for x in gathered]
    swapped += [lax.ppermute(x, "row", plan.swap()) for x in gathered[1:]]
    last = (1 << plan.stages) - 1
    outputs = []
    for masks in ([0], list(range(1, last))):
        made = [gathered[m] for m in masks], [swapped[m] for m in masks]
        done = early(plan, masks, meta, *made, held, inputs[0].shape, outputs)
        held, outputs = done[:4], done[4:]
    done = late(plan, [last], meta, gathered[last:], swapped[last:], lefts, held, outputs)
    return tuple(unflat(x, shape) for x in (done[2], done[3], done[0], done[1]))


def solution(mesh):
    spread = P(None, "row", None, "col")
    return jax.shard_map(
        shards,
        mesh=mesh,
        in_specs=(spread,) * 4 + (P(), P(), P(None, "row", None, None, None)),
        out_specs=(spread,) * 4,
        check_vma=False,
    )
```

```python
import functools
import math

import jax
import jax.numpy as jnp
import numpy as np
from jax import lax
from jax.experimental import pallas as pl
from jax.experimental.pallas import tpu as pltpu
from jax.sharding import PartitionSpec as P


F32 = jnp.float32
BF16 = jnp.bfloat16
LANES = 128
MIB = 1 << 20
ANY = pl.BlockSpec(memory_space=pl.ANY)
SMEM = pl.BlockSpec(memory_space=pltpu.SMEM)
VMEM = pl.BlockSpec(memory_space=pltpu.VMEM)


def halves(x):
    high = x.astype(BF16)
    return high, (x - high.astype(F32)).astype(BF16)


def dot(a, b):
    return jnp.dot(a, b, preferred_element_type=F32)


def dot_nt(a, b):
    return lax.dot_general(a, b, (((1,), (1,)), ((), ())), preferred_element_type=F32)


def product(a, b):
    return dot(a[0], b[0]) + (dot(a[0], b[1]) + dot(a[1], b[0]))


class Plan:
    def __init__(self, rows, cols, row_blocks, col_blocks, rounds, own, width):
        assert rows >= 4 and rows & (rows - 1) == 0
        self.rows, self.cols, self.row_blocks, self.col_blocks = rows, cols, row_blocks, col_blocks
        self.rounds, self.own, self.width, self.parts = rounds, own, width, width // LANES
        self.blocks = row_blocks * rows
        self.nodes = rows // 2
        self.stages = self.nodes.bit_length() - 1
        self.col_units = max(1, col_blocks // self.nodes)
        self.row_units = -(-row_blocks // cols)
        self.units = self.col_units + self.row_units
        self.slots = self.nodes * self.units * rounds
        self.most = [(self.nodes >> (t + 1)) * self.units * rounds for t in range(self.stages)]
        means = [m * own * rows / self.blocks * 2**t / self.nodes for t, m in enumerate(self.most)]
        self.cap = [min(m, max(1, math.ceil(x + 2.5 * math.sqrt(x)))) for m, x in zip(self.most, means)]

    def bit(self, t, core):
        return jnp.where(core == 0, 1 << (t % self.stages), 1 << ((t + 1) % self.stages))

    def mask(self, first, last, core):
        total = 0
        for t in range(first, last):
            total = total + self.bit(t, core)
        return total

    def turn(self, t):
        pairs = []
        for row in range(self.rows):
            shift = t % self.stages if row % 2 == 0 else (t + 1) % self.stages
            pairs.append((row, row ^ (2 << shift)))
        return pairs

    def swap(self):
        return [(row, row ^ 1) for row in range(self.rows)]

    def block_of(self, node, unit, core, col):
        first = ((node * self.col_blocks) // self.nodes + unit) * self.cols + col
        part = col * self.row_units + unit - self.col_units
        second = part * self.rows + 2 * node + core
        is_col = unit < self.col_units
        return is_col, jnp.where(is_col, first, jnp.clip(second, 0, self.blocks - 1)), is_col | (part < self.row_blocks)

    def present(self, t, here, node, owner, core):
        diff, away = node ^ here, owner ^ here
        ahead = (diff & self.mask(0, t, core)) == 0
        return ahead & ((diff & self.bit(t, core)) != 0) & ((away & self.mask(t, self.stages, core)) == 0)

    def overflows(self, starts):
        axes = (self.stages, 2, self.cols, self.nodes)
        stage, core, col, here = (x.reshape(-1, 1) for x in np.indices(axes).astype(np.int32))
        bits = np.array([[1 << ((t + c) % self.stages) for c in range(2)] for t in range(self.stages)], np.int32)
        before = np.array([[bits[:t, c].sum() for c in range(2)] for t in range(self.stages)], np.int32)[stage, core]
        now, after = bits[stage, core], (self.nodes - 1) & ~before
        block = starts.reshape(1, -1)
        windows = jnp.arange(starts.shape[1], dtype=jnp.int32) // (2 * self.own)
        owner = jnp.tile(windows, starts.shape[0]).reshape(1, -1)
        mine = ((owner ^ here) & after) == 0
        copies = max(1, self.nodes // self.col_blocks)
        total = 0
        for copy in range(copies):
            node = (block // self.cols // self.col_units) * copies + copy
            on = (block % self.cols == col) & (((node ^ here) & before) == 0) & (((node ^ here) & now) != 0)
            total = total + (on & mine).astype(jnp.int32)
        row, part = block % self.rows, block // self.rows
        node = row // 2
        on = (part // self.row_units == col) & (row % 2 == core)
        on = on & (((node ^ here) & before) == 0) & (((node ^ here) & now) != 0)
        total = total + (on & mine).astype(jnp.int32)
        counts = jnp.sum(total, axis=1).reshape(self.stages, -1)
        return jnp.max(counts, axis=1) > jnp.array(self.cap, jnp.int32)


SHIFT = 12


class Walk:
    def __init__(self, plan, meta, inv, stage, table):
        self.plan, self.inv, self.stage = plan, inv, stage
        self.row, self.col = meta[0], meta[1]
        self.core, self.here = self.row % 2, self.row // 2
        self.table = table
        for t in range(stage):
            self.scan(t, self.here ^ plan.bit(t, self.core), functools.partial(self.note, t))

    def note(self, t, slot, count, info):
        self.table[t, slot] = count

    def info(self, slot):
        plan = self.plan
        node = slot // (plan.units * plan.rounds)
        unit = (slot // plan.rounds) % plan.units
        turn = slot % plan.rounds
        is_col, block, valid = plan.block_of(node, unit, self.core, self.col)
        window = jnp.where(valid, self.inv[turn, block], -1)
        side = jnp.where(is_col, self.core, 0)
        return node, turn, window, side

    def scan(self, t, here, act):
        def step(slot, count):
            info = self.info(slot)
            owner = jnp.maximum(info[2], 0) // (2 * self.plan.own)
            hit = (info[2] >= 0) & self.plan.present(t, here, info[0], owner, self.core)

            @pl.when(hit)
            def _():
                act(slot, count, info)

            return count + hit.astype(jnp.int32)

        return lax.fori_loop(0, self.plan.slots, step, jnp.int32(0))

    def source(self, slot, info):
        plan = self.plan
        _, turn, window, side = info
        row = window // plan.own
        away = (row // 2) ^ self.here
        code = ((row != self.row).astype(jnp.int32) << SHIFT) + (turn * plan.own + window % plan.own) * 2 + side
        for t in range(self.stage):
            place = self.table[t, slot]
            rest = place >= plan.cap[t]
            there = ((2 + 2 * t + rest.astype(jnp.int32)) << SHIFT) + place - jnp.where(rest, plan.cap[t], 0)
            code = jnp.where((away & plan.bit(t, self.core)) != 0, there, code)
        return code


def route_kernel(plan, t, meta, inv, jobs, table):
    walk = Walk(plan, meta, inv, t, table)
    if t < plan.stages:

        def act(slot, count, info):
            jobs[1 + count] = walk.source(slot, info)

        jobs[0] = walk.scan(t, walk.here, act)
        return
    places = plan.units * plan.rounds

    def step(place, carry):
        slot = walk.here * places + place
        info = walk.info(slot)
        jobs[places + place] = info[2]
        jobs[place] = walk.source(slot, (info[0], info[1], jnp.maximum(info[2], 0), info[3]))
        return carry

    lax.fori_loop(0, places, step, 0)


def route(plan, t, meta, inv):
    size = 1 + plan.most[t] if t < plan.stages else 2 * plan.units * plan.rounds
    return pl.pallas_call(
        functools.partial(route_kernel, plan, t),
        in_specs=[SMEM, SMEM],
        out_specs=SMEM,
        out_shape=jax.ShapeDtypeStruct((size,), jnp.int32),
        scratch_shapes=[pltpu.SMEM((max(1, t), plan.slots), jnp.int32)],
        compiler_params=pltpu.CompilerParams(vmem_limit_bytes=MIB),
    )(meta, inv)


def fetch(code, sources, target, sem):
    for number, ref in enumerate(sources):

        @pl.when((code >> SHIFT) == number)
        def _(ref=ref):
            pltpu.make_async_copy(ref.at[code & ((1 << SHIFT) - 1)], target, sem).start()


def arrived(sources, target, sem):
    pltpu.make_async_copy(sources[0].at[0], target, sem).wait()


def pack_kernel(plan, t, jobs, *refs):
    sources, (first, rest, spill, sems, spill_sem) = refs[: 2 + 2 * t], refs[2 + 2 * t :]
    cap = plan.cap[t]
    count = jobs[0]

    def begin(place, carry):
        fetch(jobs[1 + place], sources, first.at[place], sems.at[place])
        return carry

    def settle(place, carry):
        arrived(sources, first.at[place], sems.at[place])
        return carry

    def over(place, carry):
        fetch(jobs[1 + place], sources, spill, spill_sem.at[0])
        arrived(sources, spill, spill_sem.at[0])
        out = pltpu.make_async_copy(spill, rest.at[place - cap], spill_sem.at[1])
        out.start()
        out.wait()
        return carry

    lax.fori_loop(0, jnp.minimum(count, cap), begin, 0)
    lax.fori_loop(cap, count, over, 0)
    lax.fori_loop(0, jnp.minimum(count, cap), settle, 0)


def pack(plan, t, jobs, sources):
    w, cap, rest = plan.width, plan.cap[t], max(1, plan.most[t] - plan.cap[t])
    return pl.pallas_call(
        functools.partial(pack_kernel, plan, t),
        in_specs=[SMEM] + [ANY] * len(sources),
        out_specs=[VMEM, ANY],
        out_shape=[jax.ShapeDtypeStruct((cap, w, w), F32), jax.ShapeDtypeStruct((rest, w, w), F32)],
        scratch_shapes=[
            pltpu.VMEM((w, w), F32),
            pltpu.SemaphoreType.DMA((cap,)),
            pltpu.SemaphoreType.DMA((2,)),
        ],
        compiler_params=pltpu.CompilerParams(vmem_limit_bytes=4 * MIB),
    )(jobs, *placed(sources))


def order(flags):
    width = flags.shape[1]
    row = lax.broadcasted_iota(jnp.int32, (width, width), 0)
    column = lax.broadcasted_iota(jnp.int32, (width, width), 1)
    wide = jnp.broadcast_to(flags, (8, width))
    earlier = dot(wide.astype(BF16), (row < column).astype(F32).astype(BF16))[0:1]
    chosen = jnp.sum(flags, axis=1, keepdims=True)
    position = lax.broadcasted_iota(jnp.int32, (1, width), 1).astype(F32)
    target = jnp.where(flags == 1.0, earlier, chosen + position - earlier)
    return (row.astype(F32) == target).astype(F32).astype(BF16)


def orders_kernel(plan, jobs, flags, out):
    places = plan.units * plan.rounds

    def step(place, carry):
        window = jnp.maximum(jobs[places + place], 0)
        out[place] = order(flags[place % plan.rounds, pl.ds(window, 1), :].astype(F32))
        return carry

    lax.fori_loop(0, places, step, 0)


def orders(plan, jobs, flags):
    return pl.pallas_call(
        functools.partial(orders_kernel, plan),
        in_specs=[SMEM, VMEM],
        out_specs=VMEM,
        out_shape=jax.ShapeDtypeStruct((plan.units * plan.rounds, plan.width, plan.width), BF16),
        compiler_params=pltpu.CompilerParams(vmem_limit_bytes=4 * MIB),
        name="orders",
    )(jobs, flags)


def compose_kernel(plan, jobs, moves, *refs):
    count = 2 + 2 * plan.stages
    sources, (cols, lefts, raw, held, sems) = refs[:count], refs[count:]
    w = plan.width
    places = plan.units * plan.rounds
    for turn in range(plan.rounds):
        for unit in range(plan.units):
            place = unit * plan.rounds + turn

            @pl.when(jobs[places + place] >= 0)
            def _(place=place):
                fetch(jobs[place], sources, raw.at[place], sems.at[place])

    row = lax.broadcasted_iota(jnp.int32, (w, w), 0)
    column = lax.broadcasted_iota(jnp.int32, (w, w), 1)
    unit_matrix = (row == column).astype(F32)
    for turn in range(plan.rounds):
        for unit in range(plan.units):
            place = unit * plan.rounds + turn

            @pl.when(jobs[places + place] >= 0)
            def _(place=place):
                arrived(sources, raw.at[place], sems.at[place])

        for unit in range(plan.units):
            place = unit * plan.rounds + turn
            there = jobs[places + place] >= 0
            factor = halves(jnp.where(there, raw[place], 0.0))
            if turn == 0:
                moved = dot_nt(unit_matrix.astype(BF16), moves[place]).astype(BF16)
                held[unit] = jnp.where(there, dot(moved, factor[0]) + dot(moved, factor[1]), unit_matrix)
            else:
                high, low = halves(held[unit])
                moved = dot_nt(high, moves[place]) + dot_nt(low, moves[place])
                held[unit] = jnp.where(there, product(halves(moved), factor), held[unit])

    for unit in range(plan.col_units):
        cols[unit] = held[unit]
    for unit in range(plan.row_units):
        lefts[unit] = held[plan.col_units + unit].T


def compose(plan, jobs, moves, sources):
    w = plan.width
    return pl.pallas_call(
        functools.partial(compose_kernel, plan),
        in_specs=[SMEM, VMEM] + [ANY] * len(sources),
        out_specs=[VMEM, VMEM],
        out_shape=[
            jax.ShapeDtypeStruct((plan.col_units, w, w), F32),
            jax.ShapeDtypeStruct((plan.row_units, w, w), F32),
        ],
        scratch_shapes=[
            pltpu.VMEM((plan.units * plan.rounds, w, w), F32),
            pltpu.VMEM((plan.units, w, w), F32),
            pltpu.SemaphoreType.DMA((plan.units * plan.rounds,)),
        ],
        compiler_params=pltpu.CompilerParams(vmem_limit_bytes=8 * MIB),
        name="compose",
    )(jobs, moves, *placed(sources))


def tiles(plan, act):
    def step(a, carry):
        for b in range(plan.col_blocks):
            for p in range(plan.parts):
                act(a, b, p)
        return carry

    lax.fori_loop(0, plan.row_blocks, step, 0)


def hbm_piece(ref, a, b, p):
    return ref.at[a, :, p, b, 0]


def vmem_piece(ref, a, b, p):
    return ref.at[a, b, :, pl.ds(p * LANES, LANES)]


def stage_kernel(plan, count, meta, *refs):
    inputs, held, rest = refs[:count], refs[count : 2 * count], refs[2 * count :]
    heights, sems = (rest[0], rest[1]) if len(rest) == 2 else (None, rest[0])

    def copy(m, a, b, p):
        sem = sems.at[m, a, b] if heights is not None else sems.at[m]
        return pltpu.make_async_copy(hbm_piece(inputs[m], a, b, p), vmem_piece(held[m], a, b, p), sem)

    for m in range(count):
        tiles(plan, lambda a, b, p, m=m: copy(m, a, b, p).start())
    if heights is None:
        for m in range(count):
            tiles(plan, lambda a, b, p, m=m: copy(m, a, b, p).wait())
        return
    for b in range(plan.col_blocks):
        heights[b] = 0

    def look(a, carry):
        for b in range(plan.col_blocks):
            for m in range(count):
                for p in range(plan.parts):
                    copy(m, a, b, p).wait()
            below = a * plan.rows + meta[0] > b * plan.cols + meta[1]

            @pl.when(jnp.logical_not(below))
            def _(b=b):
                heights[b] = a + 1

            @pl.when(below)
            def _(b=b):
                top = jnp.abs(held[0][a, b])
                for m in range(1, count):
                    top = jnp.maximum(top, jnp.abs(held[m][a, b]))

                @pl.when(jnp.max(top) > 0.0)
                def _():
                    heights[b] = a + 1

        return carry

    lax.fori_loop(0, plan.row_blocks, look, 0)


def stage(plan, meta, inputs, heights):
    shape = (plan.row_blocks, plan.col_blocks, plan.width, plan.width)
    count = len(inputs)
    extra = [jax.ShapeDtypeStruct((plan.col_blocks,), jnp.int32)] if heights else []
    return pl.pallas_call(
        functools.partial(stage_kernel, plan, count),
        in_specs=[SMEM] + [ANY] * count,
        out_specs=[VMEM] * count + [SMEM] * len(extra),
        out_shape=[pltpu.VMEM(shape, F32)] * count + extra,
        scratch_shapes=[pltpu.SemaphoreType.DMA((count,) + (shape[:2] if heights else ()))],
        compiler_params=pltpu.CompilerParams(vmem_limit_bytes=MIB),
    )(meta, *in_hbm(inputs))


def combine(plan, m, core):
    offset = 0
    for t in range(plan.stages):
        if (m >> t) & 1:
            offset = offset ^ plan.bit(t, core)
    return offset


def write_out(plan, source, target, b, sem):
    for a in range(plan.row_blocks):
        for p in range(plan.parts):
            pltpu.make_async_copy(vmem_piece(source, a, b, p), hbm_piece(target, a, b, p), sem).start()


def settle_out(plan, source, target, count, sem):
    def step(index, carry):
        for a in range(plan.row_blocks):
            for p in range(plan.parts):
                pltpu.make_async_copy(vmem_piece(source, a, 0, p), hbm_piece(target, a, 0, p), sem).wait()
        return carry

    lax.fori_loop(0, count, step, 0)


def by_height(plan, height, act):
    for count in range(1, plan.row_blocks + 1):

        @pl.when(height == count)
        def _(count=count):
            act(count)


def columns(plan, masks, meta, heights, gathered, swapped, data, outputs, high, low, places, sem):
    core, here = meta[0] % 2, meta[0] // 2
    count = jnp.int32(0)
    slots = {}
    for index, m in enumerate(masks):
        node = here ^ combine(plan, m, core)
        base = (node * plan.col_blocks) // plan.nodes
        whole = (node * plan.col_blocks) % plan.nodes == 0
        for unit in range(plan.col_units):
            places[count] = base + unit
            slots[index, unit] = count
            h, l = halves(gathered[index][unit])
            high[core, base + unit] = h
            low[core, base + unit] = l
            count = count + whole.astype(jnp.int32)
        other = here ^ combine(plan, m, 1 - core)
        base = (other * plan.col_blocks) // plan.nodes
        for unit in range(plan.col_units):
            h, l = halves(swapped[index][unit])
            high[1 - core, base + unit] = h
            low[1 - core, base + unit] = l

    def step(index, carry):
        b = places[index]
        for m, kind in ((2, 0), (3, 1)):
            ref = data[m]
            for a in range(plan.row_blocks):
                ref[a, b] = product(halves(ref[a, b]), (high[kind, b], low[kind, b]))
            write_out(plan, ref, outputs[m - 2], b, sem)

        def pencil(height):
            for a in range(height):
                for m in range(2):
                    data[m][a, b] = product(halves(data[m][a, b]), (high[1, b], low[1, b]))

        by_height(plan, heights[b], pencil)
        return carry

    lax.fori_loop(0, count, step, 0)
    return count


def early_kernel(plan, masks, extra, meta, heights, *refs):
    n = len(masks)
    gathered, swapped, refs = refs[:n], refs[n : 2 * n], refs[2 * n + 4 + extra :]
    data, outputs, (high, low, places, sem) = refs[:4], refs[4:6], refs[6:]
    count = columns(plan, masks, meta, heights, gathered, swapped, data, outputs, high, low, places, sem)
    settle_out(plan, data[2], outputs[0], 2 * count, sem)


def late_kernel(plan, masks, meta, heights, *refs):
    n, br = len(masks), plan.row_blocks
    gathered, swapped, refs = refs[:n], refs[n : 2 * n], refs[2 * n :]
    lefts, refs = refs[: plan.cols], refs[plan.cols + 6 :]
    data, outputs, refs = refs[:4], refs[4:8], refs[8:]
    high, low, places, left, sem = refs
    w = plan.width
    for shift in range(plan.cols):
        origin = (meta[1] + plan.cols - shift) % plan.cols
        for unit in range(plan.row_units):
            place = origin * plan.row_units + unit

            @pl.when(place < br)
            def _(shift=shift, unit=unit, place=place):
                h, l = halves(lefts[shift][unit])
                left[place, pl.ds(0, plan.width)] = h
                left[place, pl.ds(plan.width, plan.width)] = l

    count = columns(plan, masks, meta, heights, gathered, swapped, data, outputs[:2], high, low, places, sem)

    def rows(b, carry):
        def pencil(height):
            for a in range(height):
                for m in range(2):
                    y = halves(data[m][a, b])
                    both = dot(left[a], y[0])
                    data[m][a, b] = both[:w] + (both[w:] + dot(left[a, :w], y[1]))

        by_height(plan, heights[b], pencil)
        for m in range(2):
            write_out(plan, data[m], outputs[2 + m], b, sem)
        return carry

    lax.fori_loop(0, plan.col_blocks, rows, 0)
    settle_out(plan, data[0], outputs[2], 2 * count + 2 * plan.col_blocks, sem)


def held_in_vmem(xs):
    return [pltpu.with_memory_space_constraint(x, pltpu.VMEM) for x in xs]


def placed(sources):
    spaces = [pltpu.VMEM if i >= 2 and i % 2 == 0 else pltpu.HBM for i in range(len(sources))]
    return [pltpu.with_memory_space_constraint(x, space) for x, space in zip(sources, spaces)]


def in_hbm(xs):
    return [pltpu.with_memory_space_constraint(x, pltpu.HBM) for x in xs]


def scratch(plan, limit):
    w, bc = plan.width, plan.col_blocks
    return [
        pltpu.VMEM((2, bc, w, w), BF16),
        pltpu.VMEM((2, bc, w, w), BF16),
        pltpu.SMEM((limit + 1,), jnp.int32),
    ]


def early(plan, masks, meta, heights, gathered, swapped, data, shape, outputs):
    n = len(masks)
    held = [pltpu.VMEM(data[0].shape, F32)] * 4
    return pl.pallas_call(
        functools.partial(early_kernel, plan, masks, len(outputs)),
        in_specs=[SMEM, SMEM] + [VMEM] * (2 * n + 4) + [ANY] * len(outputs),
        out_specs=[VMEM] * 4 + [ANY] * 2,
        out_shape=held + [jax.ShapeDtypeStruct(shape, F32)] * 2,
        input_output_aliases={2 + 2 * n + i: i for i in range(4 + len(outputs))},
        scratch_shapes=scratch(plan, n * plan.col_units) + [pltpu.SemaphoreType.DMA(())],
        compiler_params=pltpu.CompilerParams(vmem_limit_bytes=8 * MIB),
    )(meta, heights, *gathered, *swapped, *held_in_vmem(data), *in_hbm(outputs))


def late(plan, masks, meta, heights, gathered, swapped, lefts, data, outputs):
    n, w = len(masks), plan.width
    first = 2 + 2 * n + len(lefts)
    held = [pltpu.VMEM(data[0].shape, F32)] * 4
    shape = jax.ShapeDtypeStruct(outputs[0].shape, F32)
    return pl.pallas_call(
        functools.partial(late_kernel, plan, masks),
        in_specs=[SMEM, SMEM] + [VMEM] * (2 * n + len(lefts) + 4) + [ANY] * 2,
        out_specs=[VMEM] * 4 + [ANY] * 4,
        out_shape=held + [shape] * 4,
        input_output_aliases={first + i: i for i in range(6)},
        scratch_shapes=scratch(plan, n * plan.col_units)
        + [pltpu.VMEM((plan.row_blocks, 2 * w, w), BF16)]
        + [pltpu.SemaphoreType.DMA(())],
        compiler_params=pltpu.CompilerParams(vmem_limit_bytes=8 * MIB),
        name="late",
    )(meta, heights, *gathered, *swapped, *lefts, *held_in_vmem(data), *in_hbm(outputs))[4:]


def flat(x):
    a, q, b, m = x.shape
    return x.reshape(a, q, b, m // LANES, LANES).transpose(0, 1, 3, 2, 4).reshape(a, q, m // LANES, b, 1, LANES)


def unflat(y, shape):
    a, q, b, m = shape
    return y.reshape(a, q, m // LANES, b, LANES).transpose(0, 1, 3, 2, 4).reshape(shape)


def shards(upper_s, upper_t, left_vectors, right_vectors, window_starts, selection, window_factors):
    rows, cols = lax.axis_size("row"), lax.axis_size("col")
    shape = upper_s.shape
    plan = Plan(rows, cols, shape[0], shape[2], window_starts.shape[0], window_factors.shape[1], shape[1])
    meta = jnp.stack([lax.axis_index("row"), lax.axis_index("col")]).astype(jnp.int32)
    numbers = jnp.arange(plan.blocks, dtype=jnp.int32)
    windows = jnp.arange(window_starts.shape[1], dtype=jnp.int32)
    same = window_starts[:, None, :] == numbers[None, :, None]
    inv = jnp.sum(jnp.where(same, windows + 1, 0), axis=2) - 1
    over = plan.overflows(window_starts)

    inputs = [flat(x) for x in (upper_s, upper_t, left_vectors, right_vectors)]
    return steps(plan, meta, inv, over, inputs, shape, selection, window_factors)


def steps(plan, meta, inv, over, inputs, shape, selection, window_factors):
    cols = plan.cols
    *held, heights = stage(plan, meta, inputs[:2], True)
    held = held + list(stage(plan, meta, inputs[2:], False))
    window_factors = window_factors.reshape((-1,) + window_factors.shape[3:])
    sources = [window_factors, lax.ppermute(window_factors, "row", plan.swap())]
    for t in range(plan.stages):
        first, rest = pack(plan, t, route(plan, t, meta, inv), sources)
        sent = functools.partial(lax.ppermute, axis_name="row", perm=plan.turn(t))
        moved = sent(first)
        sources += [moved, lax.cond(over[t], sent, lambda x: x, rest)]
    jobs = route(plan, plan.stages, meta, inv)
    moves = orders(plan, jobs, selection)
    made, left = compose(plan, jobs, moves, sources)

    lefts = [left]
    for shift in range(1, cols):
        lefts.append(lax.ppermute(left, "col", [(c, (c + shift) % cols) for c in range(cols)]))
    gathered = [made]
    swapped = [lax.ppermute(made, "row", plan.swap())]
    for t in range(plan.stages):
        gathered += [lax.ppermute(x, "row", plan.turn(t)) for x in gathered]
    swapped += [lax.ppermute(x, "row", plan.swap()) for x in gathered[1:]]
    last = (1 << plan.stages) - 1
    outputs = []
    for masks in ([0], list(range(1, last))):
        made = [gathered[m] for m in masks], [swapped[m] for m in masks]
        done = early(plan, masks, meta, heights, *made, held, inputs[0].shape, outputs)
        held, outputs = done[:4], done[4:]
    done = late(plan, [last], meta, heights, gathered[last:], swapped[last:], lefts, held, outputs)
    return tuple(unflat(x, shape) for x in (done[2], done[3], done[0], done[1]))


def solution(mesh):
    spread = P(None, "row", None, "col")
    return jax.shard_map(
        shards,
        mesh=mesh,
        in_specs=(spread,) * 4 + (P(), P(), P(None, "row", None, None, None)),
        out_specs=(spread,) * 4,
        check_vma=False,
    )
```

```python
import functools
import math

import jax
import jax.numpy as jnp
import numpy as np
from jax import lax
from jax.experimental import pallas as pl
from jax.experimental.pallas import tpu as pltpu
from jax.sharding import PartitionSpec as P


F32 = jnp.float32
BF16 = jnp.bfloat16
LANES = 128
MIB = 1 << 20
ANY = pl.BlockSpec(memory_space=pl.ANY)
SMEM = pl.BlockSpec(memory_space=pltpu.SMEM)
VMEM = pl.BlockSpec(memory_space=pltpu.VMEM)


def halves(x):
    high = x.astype(BF16)
    return high, (x - high.astype(F32)).astype(BF16)


def dot(a, b):
    return jnp.dot(a, b, preferred_element_type=F32)


def dot_nt(a, b):
    return lax.dot_general(a, b, (((1,), (1,)), ((), ())), preferred_element_type=F32)


def product(a, b):
    return dot(a[0], b[0]) + (dot(a[0], b[1]) + dot(a[1], b[0]))


class Plan:
    def __init__(self, rows, cols, row_blocks, col_blocks, rounds, own, width):
        assert rows >= 4 and rows & (rows - 1) == 0
        self.rows, self.cols, self.row_blocks, self.col_blocks = rows, cols, row_blocks, col_blocks
        self.rounds, self.own, self.width, self.parts = rounds, own, width, width // LANES
        self.blocks = row_blocks * rows
        self.nodes = rows // 2
        self.stages = self.nodes.bit_length() - 1
        self.col_units = max(1, col_blocks // self.nodes)
        self.row_units = -(-row_blocks // cols)
        self.units = self.col_units + self.row_units
        self.slots = self.nodes * self.units * rounds
        self.most = [(self.nodes >> (t + 1)) * self.units * rounds for t in range(self.stages)]
        means = [m * own * rows / self.blocks * 2**t / self.nodes for t, m in enumerate(self.most)]
        self.cap = [min(m, max(1, math.ceil(x + 2.5 * math.sqrt(x)))) for m, x in zip(self.most, means)]

    def bit(self, t, core):
        return jnp.where(core == 0, 1 << (t % self.stages), 1 << ((t + 1) % self.stages))

    def mask(self, first, last, core):
        total = 0
        for t in range(first, last):
            total = total + self.bit(t, core)
        return total

    def turn(self, t):
        pairs = []
        for row in range(self.rows):
            shift = t % self.stages if row % 2 == 0 else (t + 1) % self.stages
            pairs.append((row, row ^ (2 << shift)))
        return pairs

    def swap(self):
        return [(row, row ^ 1) for row in range(self.rows)]

    def block_of(self, node, unit, core, col):
        first = ((node * self.col_blocks) // self.nodes + unit) * self.cols + col
        part = col * self.row_units + unit - self.col_units
        second = part * self.rows + 2 * node + core
        is_col = unit < self.col_units
        return is_col, jnp.where(is_col, first, jnp.clip(second, 0, self.blocks - 1)), is_col | (part < self.row_blocks)

    def present(self, t, here, node, owner, core):
        diff, away = node ^ here, owner ^ here
        ahead = (diff & self.mask(0, t, core)) == 0
        return ahead & ((diff & self.bit(t, core)) != 0) & ((away & self.mask(t, self.stages, core)) == 0)

    def overflows(self, starts):
        axes = (self.stages, 2, self.cols, self.nodes)
        stage, core, col, here = (x.reshape(-1, 1) for x in np.indices(axes).astype(np.int32))
        bits = np.array([[1 << ((t + c) % self.stages) for c in range(2)] for t in range(self.stages)], np.int32)
        before = np.array([[bits[:t, c].sum() for c in range(2)] for t in range(self.stages)], np.int32)[stage, core]
        now, after = bits[stage, core], (self.nodes - 1) & ~before
        block = starts.reshape(1, -1)
        windows = jnp.arange(starts.shape[1], dtype=jnp.int32) // (2 * self.own)
        owner = jnp.tile(windows, starts.shape[0]).reshape(1, -1)
        mine = ((owner ^ here) & after) == 0
        copies = max(1, self.nodes // self.col_blocks)
        total = 0
        for copy in range(copies):
            node = (block // self.cols // self.col_units) * copies + copy
            on = (block % self.cols == col) & (((node ^ here) & before) == 0) & (((node ^ here) & now) != 0)
            total = total + (on & mine).astype(jnp.int32)
        row, part = block % self.rows, block // self.rows
        node = row // 2
        on = (part // self.row_units == col) & (row % 2 == core)
        on = on & (((node ^ here) & before) == 0) & (((node ^ here) & now) != 0)
        total = total + (on & mine).astype(jnp.int32)
        counts = jnp.sum(total, axis=1).reshape(self.stages, -1)
        return jnp.max(counts, axis=1) > jnp.array(self.cap, jnp.int32)


SHIFT = 12


class Walk:
    def __init__(self, plan, meta, inv, stage, table):
        self.plan, self.inv, self.stage = plan, inv, stage
        self.row, self.col = meta[0], meta[1]
        self.core, self.here = self.row % 2, self.row // 2
        self.table = table
        for t in range(stage):
            self.scan(t, self.here ^ plan.bit(t, self.core), functools.partial(self.note, t))

    def note(self, t, slot, count, info):
        self.table[t, slot] = count

    def info(self, slot):
        plan = self.plan
        node = slot // (plan.units * plan.rounds)
        unit = (slot // plan.rounds) % plan.units
        turn = slot % plan.rounds
        is_col, block, valid = plan.block_of(node, unit, self.core, self.col)
        window = jnp.where(valid, self.inv[turn, block], -1)
        side = jnp.where(is_col, self.core, 0)
        return node, turn, window, side

    def scan(self, t, here, act):
        def step(slot, count):
            info = self.info(slot)
            owner = jnp.maximum(info[2], 0) // (2 * self.plan.own)
            hit = (info[2] >= 0) & self.plan.present(t, here, info[0], owner, self.core)

            @pl.when(hit)
            def _():
                act(slot, count, info)

            return count + hit.astype(jnp.int32)

        return lax.fori_loop(0, self.plan.slots, step, jnp.int32(0))

    def source(self, slot, info):
        plan = self.plan
        _, turn, window, side = info
        row = window // plan.own
        away = (row // 2) ^ self.here
        code = ((row != self.row).astype(jnp.int32) << SHIFT) + (turn * plan.own + window % plan.own) * 2 + side
        for t in range(self.stage):
            place = self.table[t, slot]
            rest = place >= plan.cap[t]
            there = ((2 + 2 * t + rest.astype(jnp.int32)) << SHIFT) + place - jnp.where(rest, plan.cap[t], 0)
            code = jnp.where((away & plan.bit(t, self.core)) != 0, there, code)
        return code


def route_kernel(plan, t, meta, inv, jobs, table):
    walk = Walk(plan, meta, inv, t, table)
    if t < plan.stages:

        def act(slot, count, info):
            jobs[1 + count] = walk.source(slot, info)

        jobs[0] = walk.scan(t, walk.here, act)
        return
    places = plan.units * plan.rounds

    def step(place, carry):
        slot = walk.here * places + place
        info = walk.info(slot)
        jobs[places + place] = info[2]
        jobs[place] = walk.source(slot, (info[0], info[1], jnp.maximum(info[2], 0), info[3]))
        return carry

    lax.fori_loop(0, places, step, 0)


def route(plan, t, meta, inv):
    size = 1 + plan.most[t] if t < plan.stages else 2 * plan.units * plan.rounds
    return pl.pallas_call(
        functools.partial(route_kernel, plan, t),
        in_specs=[SMEM, SMEM],
        out_specs=SMEM,
        out_shape=jax.ShapeDtypeStruct((size,), jnp.int32),
        scratch_shapes=[pltpu.SMEM((max(1, t), plan.slots), jnp.int32)],
        compiler_params=pltpu.CompilerParams(vmem_limit_bytes=MIB),
    )(meta, inv)


def fetch(code, sources, target, sem):
    for number, ref in enumerate(sources):

        @pl.when((code >> SHIFT) == number)
        def _(ref=ref):
            pltpu.make_async_copy(ref.at[code & ((1 << SHIFT) - 1)], target, sem).start()


def arrived(sources, target, sem):
    pltpu.make_async_copy(sources[0].at[0], target, sem).wait()


def pack_kernel(plan, t, jobs, *refs):
    sources, (first, rest, spill, sems, spill_sem) = refs[: 2 + 2 * t], refs[2 + 2 * t :]
    cap = plan.cap[t]
    count = jobs[0]

    def begin(place, carry):
        fetch(jobs[1 + place], sources, first.at[place], sems.at[place])
        return carry

    def settle(place, carry):
        arrived(sources, first.at[place], sems.at[place])
        return carry

    def over(place, carry):
        fetch(jobs[1 + place], sources, spill, spill_sem.at[0])
        arrived(sources, spill, spill_sem.at[0])
        out = pltpu.make_async_copy(spill, rest.at[place - cap], spill_sem.at[1])
        out.start()
        out.wait()
        return carry

    lax.fori_loop(0, jnp.minimum(count, cap), begin, 0)
    lax.fori_loop(cap, count, over, 0)
    lax.fori_loop(0, jnp.minimum(count, cap), settle, 0)


def pack(plan, t, jobs, sources):
    w, cap, rest = plan.width, plan.cap[t], max(1, plan.most[t] - plan.cap[t])
    return pl.pallas_call(
        functools.partial(pack_kernel, plan, t),
        in_specs=[SMEM] + [ANY] * len(sources),
        out_specs=[VMEM, ANY],
        out_shape=[jax.ShapeDtypeStruct((cap, w, w), F32), jax.ShapeDtypeStruct((rest, w, w), F32)],
        scratch_shapes=[
            pltpu.VMEM((w, w), F32),
            pltpu.SemaphoreType.DMA((cap,)),
            pltpu.SemaphoreType.DMA((2,)),
        ],
        compiler_params=pltpu.CompilerParams(vmem_limit_bytes=4 * MIB),
    )(jobs, *placed(sources))


def order(flags):
    width = flags.shape[1]
    row = lax.broadcasted_iota(jnp.int32, (width, width), 0)
    column = lax.broadcasted_iota(jnp.int32, (width, width), 1)
    wide = jnp.broadcast_to(flags, (8, width))
    earlier = dot(wide.astype(BF16), (row < column).astype(F32).astype(BF16))[0:1]
    chosen = jnp.sum(flags, axis=1, keepdims=True)
    position = lax.broadcasted_iota(jnp.int32, (1, width), 1).astype(F32)
    target = jnp.where(flags == 1.0, earlier, chosen + position - earlier)
    return (row.astype(F32) == target).astype(F32).astype(BF16)


def orders_kernel(plan, jobs, flags, out):
    places = plan.units * plan.rounds

    def step(place, carry):
        window = jnp.maximum(jobs[places + place], 0)
        out[place] = order(flags[place % plan.rounds, pl.ds(window, 1), :].astype(F32))
        return carry

    lax.fori_loop(0, places, step, 0)


def orders(plan, jobs, flags):
    return pl.pallas_call(
        functools.partial(orders_kernel, plan),
        in_specs=[SMEM, VMEM],
        out_specs=VMEM,
        out_shape=jax.ShapeDtypeStruct((plan.units * plan.rounds, plan.width, plan.width), BF16),
        compiler_params=pltpu.CompilerParams(vmem_limit_bytes=4 * MIB),
        name="orders",
    )(jobs, flags)


def compose_kernel(plan, jobs, moves, *refs):
    count = 2 + 2 * plan.stages
    sources, (cols, lefts, raw, held, sems) = refs[:count], refs[count:]
    w = plan.width
    places = plan.units * plan.rounds
    for turn in range(plan.rounds):
        for unit in range(plan.units):
            place = unit * plan.rounds + turn

            @pl.when(jobs[places + place] >= 0)
            def _(place=place):
                fetch(jobs[place], sources, raw.at[place], sems.at[place])

    row = lax.broadcasted_iota(jnp.int32, (w, w), 0)
    column = lax.broadcasted_iota(jnp.int32, (w, w), 1)
    unit_matrix = (row == column).astype(F32)
    for turn in range(plan.rounds):
        for unit in range(plan.units):
            place = unit * plan.rounds + turn

            @pl.when(jobs[places + place] >= 0)
            def _(place=place):
                arrived(sources, raw.at[place], sems.at[place])

        for unit in range(plan.units):
            place = unit * plan.rounds + turn
            there = jobs[places + place] >= 0
            factor = halves(jnp.where(there, raw[place], 0.0))
            if turn == 0:
                moved = dot_nt(unit_matrix.astype(BF16), moves[place]).astype(BF16)
                held[unit] = jnp.where(there, dot(moved, factor[0]) + dot(moved, factor[1]), unit_matrix)
            else:
                high, low = halves(held[unit])
                moved = dot_nt(high, moves[place]) + dot_nt(low, moves[place])
                held[unit] = jnp.where(there, product(halves(moved), factor), held[unit])

    for unit in range(plan.col_units):
        cols[unit] = held[unit]
    for unit in range(plan.row_units):
        lefts[unit] = held[plan.col_units + unit].T


def compose(plan, jobs, moves, sources):
    w = plan.width
    return pl.pallas_call(
        functools.partial(compose_kernel, plan),
        in_specs=[SMEM, VMEM] + [ANY] * len(sources),
        out_specs=[VMEM, VMEM],
        out_shape=[
            jax.ShapeDtypeStruct((plan.col_units, w, w), F32),
            jax.ShapeDtypeStruct((plan.row_units, w, w), F32),
        ],
        scratch_shapes=[
            pltpu.VMEM((plan.units * plan.rounds, w, w), F32),
            pltpu.VMEM((plan.units, w, w), F32),
            pltpu.SemaphoreType.DMA((plan.units * plan.rounds,)),
        ],
        compiler_params=pltpu.CompilerParams(vmem_limit_bytes=8 * MIB),
        name="compose",
    )(jobs, moves, *placed(sources))


def tiles(plan, act):
    def step(a, carry):
        for b in range(plan.col_blocks):
            for p in range(plan.parts):
                act(a, b, p)
        return carry

    lax.fori_loop(0, plan.row_blocks, step, 0)


def hbm_piece(ref, a, b, p):
    return ref.at[a, :, p, b, 0]


def vmem_piece(ref, a, b, p):
    return ref.at[a, b, :, pl.ds(p * LANES, LANES)]


def stage_kernel(plan, count, meta, *refs):
    inputs, held, rest = refs[:count], refs[count : 2 * count], refs[2 * count :]
    heights, sems = (rest[0], rest[1]) if len(rest) == 2 else (None, rest[0])

    def copy(m, a, b, p):
        sem = sems.at[m, a, b] if heights is not None else sems.at[m]
        return pltpu.make_async_copy(hbm_piece(inputs[m], a, b, p), vmem_piece(held[m], a, b, p), sem)

    for m in range(count):
        tiles(plan, lambda a, b, p, m=m: copy(m, a, b, p).start())
    if heights is None:
        for m in range(count):
            tiles(plan, lambda a, b, p, m=m: copy(m, a, b, p).wait())
        return
    for b in range(plan.col_blocks):
        heights[b] = 0

    def look(a, carry):
        for b in range(plan.col_blocks):
            for m in range(count):
                for p in range(plan.parts):
                    copy(m, a, b, p).wait()
            below = a * plan.rows + meta[0] > b * plan.cols + meta[1]

            @pl.when(jnp.logical_not(below))
            def _(b=b):
                heights[b] = a + 1

            @pl.when(below)
            def _(b=b):
                top = jnp.abs(held[0][a, b])
                for m in range(1, count):
                    top = jnp.maximum(top, jnp.abs(held[m][a, b]))

                @pl.when(jnp.max(top) > 0.0)
                def _():
                    heights[b] = a + 1

        return carry

    lax.fori_loop(0, plan.row_blocks, look, 0)


def stage(plan, meta, inputs, heights):
    shape = (plan.row_blocks, plan.col_blocks, plan.width, plan.width)
    count = len(inputs)
    extra = [jax.ShapeDtypeStruct((plan.col_blocks,), jnp.int32)] if heights else []
    return pl.pallas_call(
        functools.partial(stage_kernel, plan, count),
        in_specs=[SMEM] + [ANY] * count,
        out_specs=[VMEM] * count + [SMEM] * len(extra),
        out_shape=[pltpu.VMEM(shape, F32)] * count + extra,
        scratch_shapes=[pltpu.SemaphoreType.DMA((count,) + (shape[:2] if heights else ()))],
        compiler_params=pltpu.CompilerParams(vmem_limit_bytes=MIB),
    )(meta, *in_hbm(inputs))


def combine(plan, m, core):
    offset = 0
    for t in range(plan.stages):
        if (m >> t) & 1:
            offset = offset ^ plan.bit(t, core)
    return offset


def write_out(plan, source, target, b, sem):
    for a in range(plan.row_blocks):
        for p in range(plan.parts):
            pltpu.make_async_copy(vmem_piece(source, a, b, p), hbm_piece(target, a, b, p), sem).start()


def settle_out(plan, source, target, count, sem):
    def step(index, carry):
        for a in range(plan.row_blocks):
            for p in range(plan.parts):
                pltpu.make_async_copy(vmem_piece(source, a, 0, p), hbm_piece(target, a, 0, p), sem).wait()
        return carry

    lax.fori_loop(0, count, step, 0)


def tallest(heights, first, count):
    top = heights[first]
    for step in range(1, count):
        top = jnp.maximum(top, heights[first + step])
    return top


def by_height(plan, height, act):
    for count in range(1, plan.row_blocks + 1):

        @pl.when(height == count)
        def _(count=count):
            act(count)


def columns(plan, masks, meta, heights, gathered, swapped, data, outputs, high, low, places, sem):
    core, here = meta[0] % 2, meta[0] // 2
    count = jnp.int32(0)
    for index, m in enumerate(masks):
        node = here ^ combine(plan, m, core)
        base = (node * plan.col_blocks) // plan.nodes
        whole = (node * plan.col_blocks) % plan.nodes == 0
        places[count] = base
        count = count + whole.astype(jnp.int32)
        for unit in range(plan.col_units):
            h, l = halves(gathered[index][unit])
            high[core, base + unit] = h
            low[core, base + unit] = l
        other = here ^ combine(plan, m, 1 - core)
        base = (other * plan.col_blocks) // plan.nodes
        for unit in range(plan.col_units):
            h, l = halves(swapped[index][unit])
            high[1 - core, base + unit] = h
            low[1 - core, base + unit] = l

    def step(index, carry):
        base = places[index]
        for unit in range(plan.col_units):
            b = base + unit
            for m, kind in ((2, 0), (3, 1)):
                ref = data[m]
                for a in range(plan.row_blocks):
                    ref[a, b] = product(halves(ref[a, b]), (high[kind, b], low[kind, b]))
                write_out(plan, ref, outputs[m - 2], b, sem)

        def pencil(height):
            for unit in range(plan.col_units):
                b = base + unit
                for a in range(height):
                    for m in range(2):
                        data[m][a, b] = product(halves(data[m][a, b]), (high[1, b], low[1, b]))

        by_height(plan, tallest(heights, base, plan.col_units), pencil)
        return carry

    lax.fori_loop(0, count, step, 0)
    return count


def early_kernel(plan, masks, extra, meta, heights, *refs):
    n = len(masks)
    gathered, swapped, refs = refs[:n], refs[n : 2 * n], refs[2 * n + 4 + extra :]
    data, outputs, (high, low, places, sem) = refs[:4], refs[4:6], refs[6:]
    count = columns(plan, masks, meta, heights, gathered, swapped, data, outputs, high, low, places, sem)
    settle_out(plan, data[2], outputs[0], 2 * plan.col_units * count, sem)


def late_kernel(plan, masks, meta, heights, *refs):
    n, br = len(masks), plan.row_blocks
    gathered, swapped, refs = refs[:n], refs[n : 2 * n], refs[2 * n :]
    lefts, refs = refs[: plan.cols], refs[plan.cols + 6 :]
    data, outputs, refs = refs[:4], refs[4:8], refs[8:]
    high, low, places, left, sem = refs
    w = plan.width
    for shift in range(plan.cols):
        origin = (meta[1] + plan.cols - shift) % plan.cols
        for unit in range(plan.row_units):
            place = origin * plan.row_units + unit

            @pl.when(place < br)
            def _(shift=shift, unit=unit, place=place):
                h, l = halves(lefts[shift][unit])
                left[place, pl.ds(0, plan.width)] = h
                left[place, pl.ds(plan.width, plan.width)] = l

    count = columns(plan, masks, meta, heights, gathered, swapped, data, outputs[:2], high, low, places, sem)

    def rows(b, carry):
        def pencil(height):
            for a in range(height):
                for m in range(2):
                    y = halves(data[m][a, b])
                    both = dot(left[a], y[0])
                    data[m][a, b] = both[:w] + (both[w:] + dot(left[a, :w], y[1]))

        by_height(plan, heights[b], pencil)
        for m in range(2):
            write_out(plan, data[m], outputs[2 + m], b, sem)
        return carry

    lax.fori_loop(0, plan.col_blocks, rows, 0)
    settle_out(plan, data[0], outputs[2], 2 * plan.col_units * count + 2 * plan.col_blocks, sem)


def held_in_vmem(xs):
    return [pltpu.with_memory_space_constraint(x, pltpu.VMEM) for x in xs]


def placed(sources):
    spaces = [pltpu.VMEM if i >= 2 and i % 2 == 0 else pltpu.HBM for i in range(len(sources))]
    return [pltpu.with_memory_space_constraint(x, space) for x, space in zip(sources, spaces)]


def in_hbm(xs):
    return [pltpu.with_memory_space_constraint(x, pltpu.HBM) for x in xs]


def scratch(plan, limit):
    w, bc = plan.width, plan.col_blocks
    return [
        pltpu.VMEM((2, bc, w, w), BF16),
        pltpu.VMEM((2, bc, w, w), BF16),
        pltpu.SMEM((limit + 1,), jnp.int32),
    ]


def early(plan, masks, meta, heights, gathered, swapped, data, shape, outputs):
    n = len(masks)
    held = [pltpu.VMEM(data[0].shape, F32)] * 4
    return pl.pallas_call(
        functools.partial(early_kernel, plan, masks, len(outputs)),
        in_specs=[SMEM, SMEM] + [VMEM] * (2 * n + 4) + [ANY] * len(outputs),
        out_specs=[VMEM] * 4 + [ANY] * 2,
        out_shape=held + [jax.ShapeDtypeStruct(shape, F32)] * 2,
        input_output_aliases={2 + 2 * n + i: i for i in range(4 + len(outputs))},
        scratch_shapes=scratch(plan, n * plan.col_units) + [pltpu.SemaphoreType.DMA(())],
        compiler_params=pltpu.CompilerParams(vmem_limit_bytes=8 * MIB),
    )(meta, heights, *gathered, *swapped, *held_in_vmem(data), *in_hbm(outputs))


def late(plan, masks, meta, heights, gathered, swapped, lefts, data, outputs):
    n, w = len(masks), plan.width
    first = 2 + 2 * n + len(lefts)
    held = [pltpu.VMEM(data[0].shape, F32)] * 4
    shape = jax.ShapeDtypeStruct(outputs[0].shape, F32)
    return pl.pallas_call(
        functools.partial(late_kernel, plan, masks),
        in_specs=[SMEM, SMEM] + [VMEM] * (2 * n + len(lefts) + 4) + [ANY] * 2,
        out_specs=[VMEM] * 4 + [ANY] * 4,
        out_shape=held + [shape] * 4,
        input_output_aliases={first + i: i for i in range(6)},
        scratch_shapes=scratch(plan, n * plan.col_units)
        + [pltpu.VMEM((plan.row_blocks, 2 * w, w), BF16)]
        + [pltpu.SemaphoreType.DMA(())],
        compiler_params=pltpu.CompilerParams(vmem_limit_bytes=8 * MIB),
        name="late",
    )(meta, heights, *gathered, *swapped, *lefts, *held_in_vmem(data), *in_hbm(outputs))[4:]


def flat(x):
    a, q, b, m = x.shape
    return x.reshape(a, q, b, m // LANES, LANES).transpose(0, 1, 3, 2, 4).reshape(a, q, m // LANES, b, 1, LANES)


def unflat(y, shape):
    a, q, b, m = shape
    return y.reshape(a, q, m // LANES, b, LANES).transpose(0, 1, 3, 2, 4).reshape(shape)


def shards(upper_s, upper_t, left_vectors, right_vectors, window_starts, selection, window_factors):
    rows, cols = lax.axis_size("row"), lax.axis_size("col")
    shape = upper_s.shape
    plan = Plan(rows, cols, shape[0], shape[2], window_starts.shape[0], window_factors.shape[1], shape[1])
    meta = jnp.stack([lax.axis_index("row"), lax.axis_index("col")]).astype(jnp.int32)
    numbers = jnp.arange(plan.blocks, dtype=jnp.int32)
    windows = jnp.arange(window_starts.shape[1], dtype=jnp.int32)
    same = window_starts[:, None, :] == numbers[None, :, None]
    inv = jnp.sum(jnp.where(same, windows + 1, 0), axis=2) - 1
    over = plan.overflows(window_starts)

    inputs = [flat(x) for x in (upper_s, upper_t, left_vectors, right_vectors)]
    return steps(plan, meta, inv, over, inputs, shape, selection, window_factors)


def steps(plan, meta, inv, over, inputs, shape, selection, window_factors):
    cols = plan.cols
    *held, heights = stage(plan, meta, inputs[:2], True)
    held = held + list(stage(plan, meta, inputs[2:], False))
    window_factors = window_factors.reshape((-1,) + window_factors.shape[3:])
    sources = [window_factors, lax.ppermute(window_factors, "row", plan.swap())]
    for t in range(plan.stages):
        first, rest = pack(plan, t, route(plan, t, meta, inv), sources)
        sent = functools.partial(lax.ppermute, axis_name="row", perm=plan.turn(t))
        moved = sent(first)
        sources += [moved, lax.cond(over[t], sent, lambda x: x, rest)]
    jobs = route(plan, plan.stages, meta, inv)
    moves = orders(plan, jobs, selection)
    made, left = compose(plan, jobs, moves, sources)

    lefts = [left]
    for shift in range(1, cols):
        lefts.append(lax.ppermute(left, "col", [(c, (c + shift) % cols) for c in range(cols)]))
    gathered = [made]
    swapped = [lax.ppermute(made, "row", plan.swap())]
    for t in range(plan.stages):
        for m in range(1 << t):
            gathered.append(lax.ppermute(gathered[m], "row", plan.turn(t)))
    swapped += [lax.ppermute(x, "row", plan.swap()) for x in gathered[1:]]
    last = (1 << plan.stages) - 1
    outputs = []
    for masks in ([0], list(range(1, last))):
        made = [gathered[m] for m in masks], [swapped[m] for m in masks]
        done = early(plan, masks, meta, heights, *made, held, inputs[0].shape, outputs)
        held, outputs = done[:4], done[4:]
    done = late(plan, [last], meta, heights, gathered[last:], swapped[last:], lefts, held, outputs)
    return tuple(unflat(x, shape) for x in (done[2], done[3], done[0], done[1]))


def solution(mesh):
    spread = P(None, "row", None, "col")
    return jax.shard_map(
        shards,
        mesh=mesh,
        in_specs=(spread,) * 4 + (P(), P(), P(None, "row", None, None, None)),
        out_specs=(spread,) * 4,
        check_vma=False,
    )
```
